256 devices in a mesh: section: 2 (over core), seq: 16 (over y, x), mp: 8 (over z).
Axes of the slice: x: 4, y: 4, z: 8, core: 2. Of those that a mesh axis runs over, the one named last changes fastest.
Arguments:
- stream: bfloat16 [2, 2048, 3584], P(None, 'seq', 'mp'), may hold values from -6 to 6
- segment_ids: int32 [2, 2048], P(None, 'seq'), may hold values from 0 to 1, never falling along the last dimension, each value on 1 to 1536 neighbouring positions
- norm_gain: bfloat16 [2, 3584], P('section'), may hold values from 0.5 to 1.5
- in_weight: bfloat16 [2, 3584, 2, 4096], P('section', None, None, 'mp'), may hold values from -0.09375 to 0.09375
- bc_weight: bfloat16 [2, 3584, 128], P('section'), may hold values from -0.09375 to 0.09375
- dt_weight: bfloat16 [2, 3584, 64], P('section', None, 'mp'), may hold values from -0.09375 to 0.09375
- dt_bias: float32 [2, 64], P('section', 'mp'), may hold values from -4 to -1
- decay_rate: float32 [2, 64], P('section', 'mp'), may hold values from 0.001 to 0.5
- conv_inner: float32 [2, 4, 4096], P('section', None, 'mp'), may hold values from -3 to 3
- conv_state: float32 [2, 4, 128], P('section'), may hold values from -3 to 3
- skip_gain: float32 [2, 64], P('section', 'mp'), may hold values from 0.5 to 1.5
- inner_gain: bfloat16 [2, 4096], P('section', 'mp'), may hold values from 0.5 to 1.5
- out_weight: bfloat16 [2, 4096, 3584], P('section', 'mp'), may hold values from -0.09375 to 0.09375
Outputs:
- hidden: bfloat16 [2, 2, 2048, 3584], P('section', None, 'seq', 'mp')
The draws below stay inside these ranges and needn't reach their ends.
Inputs may be any that keep to these rules, and one draw needn't show every extreme that they name: `segment_ids`: within each micro-batch the document numbers start at 0 and rise by one at each new document; a document has 1 to 1536 positions.
All inputs are finite; a program needn't handle non-finite values.
Results may differ from the reference program's by a relative error of at most 0.023.
Values may be sent and summed in bfloat16 or wider, within the bound.
A program may use at most 128 MiB of HBM per device.

```python
import math
import jax
import jax.numpy as jnp
import numpy as np
from jax import lax

D = 3584
HEADS = 64
HDIM = 64
STATE = 64
CONV = 4
MB = 2
SEGS = 2
TOK_DEV = 128
LEN = 2048
INNER = 4096


def level_of(stream_key, extent, split, smallest, high):
    level = 1.0
    for dim, parts in split:
        heights = jax.random.uniform(jax.random.fold_in(jax.random.fold_in(stream_key, 6), dim), (parts,), jnp.float32, smallest / len(split), high / len(split))
        level = level * jnp.repeat(jnp.exp(heights), extent[dim] // parts).reshape((-1,) + (1,) * (len(extent) - 1 - dim))
    return level


def profile(number_of, total, reach, slope):
    weights = [(1 << 20) // math.isqrt(standing ** slope) + 1 for standing in range(2, number_of + 1)]
    spare, counts = total - reach - (number_of - 1), [1] * (number_of - 1)
    while spare > 0:
        candidates = [i for i in range(number_of - 1) if counts[i] < reach]
        whole, remaining = sum([weights[i] for i in candidates]), spare
        for i in candidates:
            addition = min(reach - counts[i], max(1, remaining * weights[i] // whole), spare)
            counts[i] = counts[i] + addition
            spare = spare - addition
    return np.array([reach] + counts)


def uneven_parts(key, count, total, limit, slope):
    if count == 2:
        one = jax.random.randint(key, (), max(1, total - limit), min(limit, total - 1) + 1)
        return jnp.stack([one, total - one])
    lengths = jnp.asarray(profile(count, total, limit, slope), jnp.int32)
    couples = (count - 1) // 2
    donor, receiver = lengths[1:1 + 2 * couples:2], lengths[2:2 + 2 * couples:2]
    slack = jnp.minimum(donor - 1, limit - receiver)
    passed = jax.random.randint(jax.random.fold_in(key, 1), (couples,), 0, 1 << 20) % (slack + 1)
    lengths = lengths.at[1:1 + 2 * couples:2].set(donor - passed).at[2:2 + 2 * couples:2].set(receiver + passed)
    return lengths[jax.random.permutation(jax.random.fold_in(key, 2), count)]


def gaussian(rng, extent, scale, bound, shards=(), kind=jnp.bfloat16):
    entries = jax.random.normal(rng, extent, jnp.float32) * scale
    if len(shards) > 0:
        entries = level_of(rng, extent, shards, -0.22, 0.18) * entries
    return jnp.clip(entries, min=-bound, max=bound).astype(kind)


def setup_inputs(seed: int = 0) -> dict:
    arg_keys = jax.random.split(jax.random.key(seed), 14)
    stream = gaussian(arg_keys[0], (MB, LEN, D), 1.0, 6.0, ((1, 16), (2, 8)))
    segment_ids = jax.vmap(lambda own: jnp.searchsorted(jnp.cumsum(uneven_parts(own, SEGS, LEN, LEN // 2 + LEN // 4, 0)), jnp.arange(LEN), side="right"))(jax.random.split(arg_keys[1], MB)).reshape((MB, LEN)).astype(jnp.int32)
    norm_gain = jnp.clip(1.0 + 0.1 * jax.random.normal(arg_keys[2], (2, D), jnp.float32), 0.5, 1.5).astype(jnp.bfloat16)
    in_weight = gaussian(arg_keys[3], (2, D, 2, INNER), D ** -0.5, 0.09375, ((0, 2), (3, 8)))
    bc_weight = gaussian(arg_keys[4], (2, D, 2 * STATE), D ** -0.5, 0.09375, ((0, 2),))
    dt_weight = gaussian(arg_keys[5], (2, D, HEADS), D ** -0.5, 0.09375, ((0, 2), (2, 8)))
    dt_bias = jnp.clip(-4.0 + 3.0 * jax.random.uniform(arg_keys[6], (2, HEADS), jnp.float32) ** level_of(arg_keys[6], (2, HEADS), ((0, 2), (1, 8)), -0.2, 0.2), -4.0, -1.0)
    decay_rate = jnp.clip(jnp.exp(math.log(0.5) - 6.214608 * jax.random.uniform(arg_keys[7], (2, HEADS), jnp.float32) ** level_of(arg_keys[7], (2, HEADS), ((0, 2), (1, 8)), -0.2, 0.2)), 0.001, 0.5)
    conv_inner = gaussian(arg_keys[8], (2, CONV, INNER), CONV ** -0.5, 3.0, ((0, 2), (2, 8)), jnp.float32)
    conv_state = gaussian(arg_keys[9], (2, CONV, 2 * STATE), CONV ** -0.5, 3.0, ((0, 2),), jnp.float32)
    skip_gain = jnp.clip(1.0 + 0.1 * jax.random.normal(arg_keys[10], (2, HEADS), jnp.float32), 0.5, 1.5)
    inner_gain = jnp.clip(1.0 + 0.1 * jax.random.normal(arg_keys[11], (2, INNER), jnp.float32), 0.5, 1.5).astype(jnp.bfloat16)
    out_weight = gaussian(arg_keys[12], (2, INNER, D), INNER ** -0.5, 0.09375, ((0, 2), (1, 8)))
    return dict(stream=stream, segment_ids=segment_ids, norm_gain=norm_gain, in_weight=in_weight, bc_weight=bc_weight, dt_weight=dt_weight, dt_bias=dt_bias, decay_rate=decay_rate, conv_inner=conv_inner, conv_state=conv_state, skip_gain=skip_gain, inner_gain=inner_gain, out_weight=out_weight)


EPS = 1e-05

def norm_rows(hidden_rows, gain):
    values = hidden_rows.astype(jnp.float32)
    scale = lax.rsqrt(lax.optimization_barrier(jnp.mean(values * values, axis=-1, keepdims=True)) + EPS)
    return (values * scale * gain.astype(jnp.float32)).astype(jnp.bfloat16)

def causal_conv(padded, pad_docs, documents, taps):
    length = documents.shape[0]
    total = jnp.zeros((length, padded.shape[1]), jnp.float32)
    for offset in range(taps.shape[0]):
        match = (pad_docs[offset:offset + length] == documents)[:, None]
        term = padded[offset:offset + length].astype(jnp.float32) * taps[offset][None, :]
        total = total + jnp.where(match, term, 0.0)
    return jax.nn.silu(total).astype(jnp.bfloat16)

def block_terms(inputs, b_rows, c_rows, steps_dt, documents, prior_doc, decay_rate):
    length = documents.shape[0]
    cumlog = jnp.cumsum(-steps_dt * decay_rate[None, :], axis=0)
    places = jnp.arange(length, dtype=jnp.int32)
    same_doc = (documents[:, None] == documents[None, :]) & (places[:, None] >= places[None, :])
    gap_log = jnp.where(same_doc[:, :, None], cumlog[:, None, :] - cumlog[None, :, :], 0.0)
    decays = jnp.where(same_doc[:, :, None], jnp.exp(gap_log), 0.0)
    intersection = jnp.dot(c_rows, b_rows.T, preferred_element_type=jnp.float32)
    mixing = (decays * intersection[:, :, None] * steps_dt[None, :, :]).astype(jnp.bfloat16)
    local_out = jnp.einsum('tsh,shp->thp', mixing.astype(jnp.float32), inputs.astype(jnp.float32))
    carry_in = jnp.where((documents == prior_doc)[:, None], jnp.exp(cumlog), 0.0)
    last_doc = documents[-1]
    tail_weight = jnp.where((documents == last_doc)[:, None], jnp.exp(cumlog[-1][None, :] - cumlog), 0.0) * steps_dt
    local_state = jnp.einsum('sh,shp,sn->hpn', tail_weight, inputs.astype(jnp.float32), b_rows.astype(jnp.float32), precision=lax.Precision.HIGHEST)
    through = jnp.where(last_doc == prior_doc, jnp.exp(cumlog[-1]), 0.0)
    return (local_out, carry_in, local_state, through)

def add_carry(local_out, carry_in, c_rows, state_in, inputs, skip_gain):
    from_state = jnp.einsum('tn,hpn->thp', c_rows.astype(jnp.float32), state_in, precision=lax.Precision.HIGHEST)
    return local_out + carry_in[:, :, None] * from_state + skip_gain[None, :, None] * inputs.astype(jnp.float32)

def mixer_layer(hidden_rows, documents, norm_gain, in_weight, bc_weight, dt_weight, dt_bias, decay_rate, conv_inner, conv_state, skip_gain, inner_gain, out_weight):
    normed = norm_rows(hidden_rows, norm_gain)
    width_all = in_weight.shape[-1]
    both = jnp.dot(normed, in_weight.reshape(in_weight.shape[0], -1), preferred_element_type=jnp.float32)
    inner_raw = both[:, :width_all]
    gate_raw = both[:, width_all:]
    state_raw = jnp.dot(normed, bc_weight, preferred_element_type=jnp.float32)
    dt_raw = jnp.dot(normed, dt_weight, preferred_element_type=jnp.float32)
    joined = jnp.concatenate([inner_raw, state_raw], axis=1).astype(jnp.bfloat16)
    taps = jnp.concatenate([conv_inner, conv_state], axis=1)
    lag = taps.shape[0] - 1
    padded = jnp.concatenate([jnp.zeros((lag, joined.shape[1]), jnp.bfloat16), joined], axis=0)
    pad_docs = jnp.concatenate([jnp.zeros((lag,), jnp.int32), documents.astype(jnp.int32)], axis=0)
    mixed_in = causal_conv(padded, pad_docs, documents, taps)
    length = hidden_rows.shape[0]
    heads = width_all // HDIM
    inputs = mixed_in[:, :width_all].reshape(length, heads, HDIM)
    b_rows = mixed_in[:, width_all:width_all + STATE]
    c_rows = mixed_in[:, width_all + STATE:]
    steps_dt = jax.nn.softplus(dt_raw + dt_bias[None, :])
    blocks = length // TOK_DEV
    block_docs = documents.reshape(blocks, TOK_DEV).astype(jnp.int32)
    prior = jnp.concatenate([jnp.zeros((1,), jnp.int32), block_docs[:-1, -1]], axis=0)

    def advance(state_in, pieces):
        inp, b_blk, c_blk, dt_blk, docs, prev = pieces
        local_out, carry_in, local_state, through = block_terms(inp, b_blk, c_blk, dt_blk, docs, prev, decay_rate)
        result = add_carry(local_out, carry_in, c_blk, state_in, inp, skip_gain)
        return (through[:, None, None] * state_in + local_state, result)
    start = jnp.zeros((heads, HDIM, STATE), jnp.float32)
    pieces = (inputs.reshape(blocks, TOK_DEV, heads, HDIM), b_rows.reshape(blocks, TOK_DEV, STATE), c_rows.reshape(blocks, TOK_DEV, STATE), steps_dt.reshape(blocks, TOK_DEV, heads), block_docs, prior)
    _, results = lax.scan(advance, start, pieces)
    gated = results.reshape(length, width_all) * jax.nn.silu(gate_raw)
    scale = lax.rsqrt(lax.optimization_barrier(jnp.mean(gated * gated, axis=-1, keepdims=True)) + EPS)
    normed_inner = (gated * scale * inner_gain.astype(jnp.float32)).astype(jnp.bfloat16)
    update = jnp.dot(normed_inner, out_weight, preferred_element_type=jnp.float32)
    return (hidden_rows.astype(jnp.float32) + update).astype(jnp.bfloat16)

def reference(stream, segment_ids, norm_gain, in_weight, bc_weight, dt_weight, dt_bias, decay_rate, conv_inner, conv_state, skip_gain, inner_gain, out_weight):
    current = stream
    layers = []
    for section_index in range(2):
        current = jnp.stack([mixer_layer(current[micro_index], segment_ids[micro_index], norm_gain[section_index], in_weight[section_index], bc_weight[section_index], dt_weight[section_index], dt_bias[section_index], decay_rate[section_index], conv_inner[section_index], conv_state[section_index], skip_gain[section_index], inner_gain[section_index], out_weight[section_index]) for micro_index in range(MB)])
        layers.append(current)
    return jnp.stack(layers)
```

```python
import jax
import jax.numpy as jnp
from jax import lax
from jax.sharding import PartitionSpec as P

HDIM = 64
STATE = 64
INNER = 4096
EPS = 1e-05


def shifted(block, axis, distance):
    devices = range(lax.axis_size(axis))
    route = [(i - distance, i) for i in devices if i - distance in devices]
    return lax.ppermute(block, axis, route)


def norm_rows(hidden_rows, gain):
    values = hidden_rows.astype(jnp.float32)
    scale = lax.rsqrt(jnp.mean(values * values, axis=-1, keepdims=True) + EPS)
    return (values * scale * gain.astype(jnp.float32)).astype(jnp.bfloat16)


def causal_conv(padded, pad_docs, documents, taps):
    length = documents.shape[0]
    total = jnp.zeros((length, padded.shape[1]), jnp.float32)
    for offset in range(taps.shape[0]):
        match = (pad_docs[offset : offset + length] == documents)[:, None]
        term = padded[offset : offset + length].astype(jnp.float32) * taps[offset][None, :]
        total = total + jnp.where(match, term, 0.0)
    return jax.nn.silu(total).astype(jnp.bfloat16)


def block_terms(inputs, b_rows, c_rows, steps_dt, documents, prior_doc, decay_rate):
    length = documents.shape[0]
    cumlog = jnp.cumsum(-steps_dt * decay_rate[None, :], axis=0)
    places = jnp.arange(length, dtype=jnp.int32)
    same_doc = (documents[:, None] == documents[None, :]) & (places[:, None] >= places[None, :])
    gap = cumlog.T[:, :, None] - cumlog.T[:, None, :]
    decays = jnp.where(same_doc[None], jnp.exp(jnp.where(same_doc[None], gap, 0.0)), 0.0)
    intersection = jnp.dot(c_rows, b_rows.T, preferred_element_type=jnp.float32)
    mixing = (decays * intersection[None] * steps_dt.T[:, None, :]).astype(jnp.bfloat16)
    local_out = jnp.einsum("hts,shp->thp", mixing, inputs, preferred_element_type=jnp.float32)
    carry_in = jnp.where((documents == prior_doc)[:, None], jnp.exp(cumlog), 0.0)
    last_doc = documents[-1]
    tail_weight = (
        jnp.where((documents == last_doc)[:, None], jnp.exp(cumlog[-1][None, :] - cumlog), 0.0)
        * steps_dt
    )
    weighted = (inputs.astype(jnp.float32) * tail_weight[:, :, None]).astype(jnp.bfloat16)
    local_state = jnp.einsum("shp,sn->hpn", weighted, b_rows, preferred_element_type=jnp.float32)
    through = jnp.where(last_doc == prior_doc, jnp.exp(cumlog[-1]), 0.0)
    return (local_out, carry_in, local_state, through)


def send_pair(through, state, distance):
    high = through.astype(jnp.bfloat16)
    low = (through - high.astype(jnp.float32)).astype(jnp.bfloat16)
    lead = through.shape
    row = jnp.concatenate(
        [high[..., None, None], low[..., None, None], jnp.zeros((*lead, 1, STATE - 2), jnp.bfloat16)],
        axis=-1,
    )
    pack = shifted(jnp.concatenate([state.astype(jnp.bfloat16), row], axis=-2), "seq", distance)
    got = pack.astype(jnp.float32)
    return got[..., HDIM, 0] + got[..., HDIM, 1], got[..., :HDIM, :]


def mixer_layer(
    hidden,
    documents,
    norm_gain,
    in_weight,
    bc_weight,
    dt_weight,
    dt_bias,
    decay_rate,
    conv_inner,
    conv_state,
    skip_gain,
    inner_gain,
    out_weight,
):
    count, length, _ = hidden.shape
    whole = lax.all_gather(hidden, "mp", axis=2, tiled=True)
    normed = norm_rows(whole, norm_gain).reshape(count * length, -1)
    width_loc = in_weight.shape[-1]
    both = jnp.dot(
        normed, in_weight.reshape(in_weight.shape[0], -1), preferred_element_type=jnp.float32
    )
    inner_raw = both[:, :width_loc]
    gate_raw = both[:, width_loc:]
    state_raw = jnp.dot(normed, bc_weight, preferred_element_type=jnp.float32)
    dt_raw = jnp.dot(normed, dt_weight, preferred_element_type=jnp.float32)
    joined = jnp.concatenate([inner_raw, state_raw], axis=1).astype(jnp.bfloat16)
    joined = joined.reshape(count, length, -1)
    taps = jnp.concatenate([conv_inner, conv_state], axis=1)
    lag = taps.shape[0] - 1
    rim_rows, rim_docs = shifted((joined[:, -lag:], documents[:, -lag:]), "seq", 1)
    padded = jnp.concatenate([rim_rows, joined], axis=1)
    pad_docs = jnp.concatenate([rim_docs, documents], axis=1)
    mixed_in = jax.vmap(causal_conv, (0, 0, 0, None))(padded, pad_docs, documents, taps)
    heads = width_loc // HDIM
    inputs = mixed_in[..., :width_loc].reshape(count, length, heads, HDIM)
    b_rows = mixed_in[..., width_loc : width_loc + STATE]
    c_rows = mixed_in[..., width_loc + STATE :]
    steps_dt = jax.nn.softplus(dt_raw + dt_bias[None, :]).reshape(count, length, heads)
    local_out, carry_in, state, through = jax.vmap(block_terms, (0, 0, 0, 0, 0, 0, None))(
        inputs, b_rows, c_rows, steps_dt, documents, rim_docs[:, -1], decay_rate
    )
    through, state = send_pair(through, state, 1)
    size = lax.axis_size("seq")
    distance = 1
    while distance < size:
        earlier, before = send_pair(through, state, distance)
        state = through[..., None, None] * before + state
        through = through * earlier
        distance *= 2
    from_state = jnp.einsum(
        "mtn,mhpn->mthp", c_rows, state.astype(jnp.bfloat16), preferred_element_type=jnp.float32
    )
    results = (
        local_out
        + carry_in[..., None] * from_state
        + skip_gain[None, None, :, None] * inputs.astype(jnp.float32)
    )
    gated = results.reshape(count * length, width_loc) * jax.nn.silu(gate_raw)
    squares = lax.psum(jnp.sum(gated * gated, axis=-1), "mp")
    scale = lax.rsqrt(squares / INNER + EPS)
    gained = (gated * inner_gain.astype(jnp.float32)).astype(jnp.bfloat16)
    update = jnp.dot(gained, out_weight, preferred_element_type=jnp.float32)
    summed = lax.psum_scatter(
        update.astype(jnp.bfloat16), "mp", scatter_dimension=1, tiled=True
    ).astype(jnp.float32)
    final = hidden.reshape(count * length, -1).astype(jnp.float32) + summed * scale[:, None]
    return final.astype(jnp.bfloat16).reshape(hidden.shape)


def per_device(stream, segment_ids, *weights):
    first = lax.axis_index("section") == 0
    weights = [w[0] for w in weights]
    result = mixer_layer(stream, segment_ids, *weights)
    received = shifted(result, "section", 1)
    second = mixer_layer(received, segment_ids, *weights)
    return jnp.where(first, result, second)[None]


def solution(mesh):
    placed = (
        P(None, "seq", "mp"),
        P(None, "seq"),
        P("section", None),
        P("section", None, None, "mp"),
        P("section", None, None),
        P("section", None, "mp"),
        P("section", "mp"),
        P("section", "mp"),
        P("section", None, "mp"),
        P("section", None, None),
        P("section", "mp"),
        P("section", "mp"),
        P("section", "mp", None),
    )
    return jax.shard_map(
        per_device,
        mesh=mesh,
        in_specs=placed,
        out_specs=P("section", None, "seq", "mp"),
        check_vma=False,
    )
```

```python
import functools
import math

import jax
import jax.numpy as jnp
from jax import lax
from jax.experimental import pallas as pl
from jax.experimental.pallas import tpu as pltpu
from jax.sharding import PartitionSpec as P

HDIM = 64
STATE = 64
EPS = 1e-05
F32 = jnp.float32
BF16 = jnp.bfloat16
HIGH = lax.Precision.HIGHEST
TOK = 128
MB = 2
LAG = 16
PACK = STATE + 16


def spread(row):
    return jnp.broadcast_to(row, (TOK, TOK))


def sigmoid(value):
    return 1.0 / (1.0 + jnp.exp(-value))


def kernel(
    size,
    row_len,
    seq_len,
    stream,
    seg,
    norm_gain,
    w_in,
    w_bc,
    w_dt,
    dt_bias,
    decay_rate,
    conv_inner,
    conv_state,
    skip_gain,
    inner_gain,
    w_out,
    out,
    xin,
    gr,
    gl,
    wi,
    wb,
    wd,
    wo,
    gains,
    acc,
    accs,
    accd,
    ss,
    jn,
    halo,
    prev,
    pad,
    dpad,
    us,
    cs,
    cums,
    flats,
    inter,
    lo,
    ce,
    pkx,
    pky,
    tpk,
    cur_s,
    cur_a,
    pre_s,
    pre_a,
    gb,
    sq,
    sqr,
    upd,
    rr,
    rl,
    sr,
    sl,
    w_sem,
    x_sem,
    agr_s,
    agr_r,
    agl_s,
    agl_r,
    h_s,
    h_r,
    d_s,
    d_r,
    px_s,
    px_r,
    py_s,
    py_r,
    q_s,
    q_r,
    rsr_s,
    rsr_r,
    rsl_s,
    rsl_r,
    sx_s,
    sx_r,
):
    local = stream.shape[-1]
    width = wo.shape[0]
    state_at = width
    col_len = seq_len // row_len
    far = size // 2
    near = size - 1 - far
    section = lax.axis_index("section")
    seq = lax.axis_index("seq")
    me = lax.axis_index("mp")
    my_x = lax.rem(seq, row_len)
    my_y = lax.div(seq, row_len)

    def at_mp(index):
        return lax.rem(me + index + 2 * size, size)

    def to_mp(index):
        return {"mp": at_mp(index)}

    def remote(src, dst, send, recv, where):
        return pltpu.make_async_remote_copy(
            src_ref=src,
            dst_ref=dst,
            send_sem=send,
            recv_sem=recv,
            device_id=where,
            device_id_type=pl.DeviceIdType.MESH,
        )

    order = [0]
    for step in range(1, far + 1):
        order.append(-step)
        if step <= near:
            order.append(step)
    slot_of = {rel: index for index, rel in enumerate(order)}

    def rows_of(rel):
        return pl.ds(pl.multiple_of(at_mp(rel) * local, 64), local)

    def weight_copies(rel):
        rows = rows_of(rel)
        k = slot_of[rel]
        return [
            pltpu.make_async_copy(w_in.at[rows], wi.at[rows], w_sem.at[k, 0]),
            pltpu.make_async_copy(w_bc.at[rows], wb.at[rows], w_sem.at[k, 1]),
            pltpu.make_async_copy(w_dt.at[rows], wd.at[rows], w_sem.at[k, 2]),
        ]

    out_copy = pltpu.make_async_copy(w_out, wo, x_sem.at[1])
    for rel in order:
        for copy in weight_copies(rel):
            copy.start()
    out_copy.start()
    first_copy = pltpu.make_async_copy(stream, xin, x_sem.at[0])

    @pl.when(section == 0)
    def _():
        first_copy.start()

    barrier = pltpu.get_barrier_semaphore()
    partners = [to_mp(d) for d in range(1, size)]
    partners += [
        {"seq": my_y * row_len + lax.rem(my_x + d, row_len)} for d in range(1, row_len)
    ]
    partners += [
        {"seq": lax.rem(my_y + d, col_len) * row_len + my_x} for d in range(1, col_len)
    ]
    partners += [{"seq": lax.rem(seq + d, seq_len)} for d in (1, seq_len - 1)]
    partners += [{"section": 1 - section}]
    for where in partners:
        pl.semaphore_signal(
            barrier, inc=1, device_id=where, device_id_type=pl.DeviceIdType.MESH
        )
    pl.semaphore_wait(barrier, len(partners))

    doc_copy = remote(seg, prev, d_s, d_r, {"seq": lax.rem(seq + 1, seq_len)})

    @pl.when(seq < seq_len - 1)
    def _():
        doc_copy.start()

    @pl.when(seq == 0)
    def _():
        prev[...] = jnp.zeros_like(prev)
        halo[...] = jnp.zeros_like(halo)

    for j in range(size):
        gains[j : j + 1, :] = norm_gain[0:1, j * local : (j + 1) * local].astype(F32)

    pass_on = [
        remote(out.at[0, mb], xin.at[mb], sx_s.at[mb], sx_r.at[mb], {"section": 1 - section})
        for mb in range(MB)
    ]

    @pl.when(section == 0)
    def _():
        first_copy.wait()

    def gather_copy(side, step, mb):
        bank, send, recv = (gr, agr_s, agr_r) if side > 0 else (gl, agl_s, agl_r)
        src = xin.at[mb] if step == 0 else bank.at[step - 1, mb]
        return remote(
            src, bank.at[step, mb], send.at[step, mb], recv.at[step, mb], to_mp(side)
        )

    def project(values, rel, first):
        for copy in weight_copies(rel):
            copy.wait()
        owner = at_mp(rel)
        rows = rows_of(rel)
        wide = values.reshape(MB * TOK, local).astype(F32)
        square = jnp.sum(wide * wide, axis=1, keepdims=True).reshape(MB, TOK, 1)
        scaled = (wide * gains[pl.ds(owner, 1), :]).astype(BF16)
        block = 256
        pieces = [(acc, wi, n * block, block) for n in range(2 * width // block)]
        pieces += [(accs, wb, 0, wb.shape[1]), (accd, wd, 0, wd.shape[1])]
        for total, weight, start, count in pieces:
            term = jnp.dot(
                scaled, weight[rows, start : start + count], preferred_element_type=F32
            ).reshape(MB, TOK, count)
            if first:
                total[:, :, start : start + count] = term
            else:
                total[:, :, start : start + count] += term
        if first:
            ss[...] = square
        else:
            ss[...] += square

    for mb in range(MB):

        @pl.when(section == 1)
        def _():
            pass_on[mb].wait_recv()

        gather_copy(1, 0, mb).start()
        gather_copy(-1, 0, mb).start()
    project(xin[...], 0, True)
    for step in range(far):
        for mb in range(MB):
            gather_copy(1, step, mb).wait_recv()
            if step + 1 < far:
                gather_copy(1, step + 1, mb).start()
            if step < near:
                gather_copy(-1, step, mb).wait_recv()
                if step + 1 < near:
                    gather_copy(-1, step + 1, mb).start()
        project(gr[step], -1 - step, False)
        if step < near:
            project(gl[step], 1 + step, False)

    def halo_copy(mb):
        return remote(
            jn.at[mb, TOK - LAG : TOK],
            halo.at[mb],
            h_s.at[mb],
            h_r.at[mb],
            {"seq": lax.rem(seq + 1, seq_len)},
        )

    def join(mb, carry):
        scale = lax.rsqrt(ss[mb] / (size * local) + EPS)
        ss[mb] = scale
        jn[mb, :, :width] = (acc[mb, :, :width] * scale).astype(BF16)
        jn[mb, :, width:] = (accs[mb] * scale).astype(BF16)

        @pl.when(seq < seq_len - 1)
        def _():
            halo_copy(mb).start()

        return carry

    lax.fori_loop(0, MB, join, 0)

    heads = width // HDIM
    spread_heads = (
        lax.broadcasted_iota(jnp.int32, (heads, width), 1) // HDIM
        == lax.broadcasted_iota(jnp.int32, (heads, width), 0)
    ).astype(F32)

    def expand(value):
        return jnp.dot(value, spread_heads, precision=HIGH, preferred_element_type=F32)

    def pack_decay(decay):
        high = decay.astype(BF16).astype(F32)
        low = decay - high
        index = lax.broadcasted_iota(jnp.int32, (LAG, width), 0)
        return jnp.where(index == 0, high, jnp.where(index == 1, low, 0.0)).astype(BF16)

    def unpack_decay(block):
        both = block.astype(F32)
        return both[0:1] + both[1:2]

    def row_copy(dest, mb):
        return remote(
            pkx.at[my_x, mb],
            pkx.at[my_x, mb],
            px_s.at[dest, mb],
            px_r.at[my_x, mb],
            {"seq": my_y * row_len + dest},
        )

    def row_arrival(source, mb):
        return remote(
            pkx.at[source, mb],
            pkx.at[source, mb],
            px_s.at[source, mb],
            px_r.at[source, mb],
            {"seq": my_y * row_len + source},
        )

    def col_copy(dest, mb):
        return remote(
            tpk.at[mb],
            pky.at[my_y, mb],
            py_s.at[dest, mb],
            py_r.at[my_y, mb],
            {"seq": dest * row_len + my_x},
        )

    def col_arrival(source, mb):
        return remote(
            tpk.at[mb],
            pky.at[source, mb],
            py_s.at[source, mb],
            py_r.at[source, mb],
            {"seq": source * row_len + my_x},
        )

    @pl.when(seq > 0)
    def _():
        doc_copy.wait_recv()

    def scan_block(mb, carry):
        own_row = spread(seg[pl.ds(mb, 1), :].astype(F32))
        own_col = own_row.T
        old_col = spread(prev[pl.ds(mb, 1), :].astype(F32)).T
        dpad[0:LAG] = old_col[TOK - LAG : TOK]
        dpad[LAG : LAG + TOK] = own_col
        doc = own_col[:, 0:1]
        prior = old_col[TOK - 1 : TOK, 0:1]
        last = own_col[TOK - 1 : TOK, 0:1]

        scale = ss[mb]
        raw = accd[mb] * scale + dt_bias[...]
        steps_dt = jnp.maximum(raw, 0.0) + jnp.log1p(jnp.exp(-jnp.abs(raw)))
        places_t = lax.broadcasted_iota(jnp.int32, (TOK, TOK), 0)
        places_s = lax.broadcasted_iota(jnp.int32, (TOK, TOK), 1)
        lower = places_t >= places_s
        cumlog = jnp.dot(
            lower.astype(F32),
            -steps_dt * decay_rate[...],
            precision=HIGH,
            preferred_element_type=F32,
        )
        tail = jnp.where(doc == last, jnp.exp(cumlog[TOK - 1 : TOK] - cumlog), 0.0) * steps_dt
        carry_in = jnp.where(doc == prior, jnp.exp(cumlog), 0.0)
        tail_wide = expand(tail)
        carry_wide = expand(carry_in)
        ce[mb] = carry_wide

        @pl.when(seq > 0)
        def _():
            halo_copy(mb).wait_recv()

        pad[0:LAG] = halo[mb].astype(F32)
        pad[LAG : LAG + TOK] = jn[mb].astype(F32)
        taps = conv_inner.shape[1]
        matches = [
            dpad[LAG - taps + 1 + k : LAG - taps + 1 + k + TOK] == own_col for k in range(taps)
        ]
        mixed = []
        for j in range(pad.shape[1] // TOK):
            lanes = slice(j * TOK, (j + 1) * TOK)
            if j * TOK < state_at:
                tap = conv_inner[0, :, lanes]
            else:
                tap = conv_state[0, :, j * TOK - state_at : (j + 1) * TOK - state_at]
            total = jnp.zeros((TOK, TOK), F32)
            for k in range(taps):
                start = LAG - taps + 1 + k
                term = pad[start : start + TOK, lanes] * tap[k : k + 1]
                total = total + jnp.where(matches[k], term, 0.0)
            mixed.append(total * sigmoid(total))
        inputs = [part.astype(BF16) for part in mixed[:-1]]
        both = mixed[-1].astype(BF16).astype(F32)
        b_cols = both.T[0:STATE].astype(BF16)
        c_rows = pltpu.roll(both, STATE, axis=1)[:, 0:STATE].astype(BF16)
        cs[mb] = c_rows
        cums[mb] = cumlog
        flats[mb] = jnp.concatenate(
            [cumlog, steps_dt, jnp.zeros((TOK, TOK - 2 * heads), F32)], axis=1
        ).T

        for j, part in enumerate(inputs):
            lanes = slice(j * TOK, (j + 1) * TOK)
            us[mb, :, lanes] = part
            weighted = (part.astype(F32) * tail_wide[:, lanes]).astype(BF16)
            pkx[my_x, mb, 0:STATE, lanes] = jnp.dot(
                b_cols, weighted, preferred_element_type=F32
            ).astype(BF16)
        pkx[my_x, mb, STATE:PACK, :] = pack_decay(carry_wide[TOK - 1 : TOK])
        for d in range(1, row_len):
            row_copy(lax.rem(my_x + d, row_len), mb).start()
        inter[mb] = jnp.where(
            lower & (own_col == own_row),
            jnp.dot(c_rows, b_cols, preferred_element_type=F32),
            0.0,
        )
        return carry

    lax.fori_loop(0, MB, scan_block, 0)
    skip_wide = expand(skip_gain[...])

    def local_block(mb, carry):
        own_row = spread(seg[pl.ds(mb, 1), :].astype(F32))
        lower = lax.broadcasted_iota(jnp.int32, (TOK, TOK), 0) >= lax.broadcasted_iota(
            jnp.int32, (TOK, TOK), 1
        )
        keep = lower & (own_row.T == own_row)
        left = lax.broadcasted_iota(jnp.int32, (TOK, TOK), 1) < HDIM
        cross = inter[mb]
        for j in range(width // TOK):
            lanes = slice(j * TOK, (j + 1) * TOK)
            mixing = []
            for h in (2 * j, 2 * j + 1):
                gap = cums[mb, :, h : h + 1] - flats[mb, h : h + 1, :]
                decays = jnp.exp(jnp.where(keep, gap, -1e30))
                mixing.append(
                    (decays * cross * flats[mb, heads + h : heads + h + 1, :]).astype(BF16)
                )
            part = us[mb, :, lanes]
            zero = jnp.zeros_like(part)
            stacked = jnp.concatenate(
                [jnp.where(left, part, zero), jnp.where(left, zero, part)], axis=0
            )
            lo[mb, :, lanes] = (
                jnp.dot(
                    jnp.concatenate(mixing, axis=1), stacked, preferred_element_type=F32
                )
                + skip_wide[:, lanes] * part.astype(F32)
            )
        return carry

    lax.fori_loop(0, MB, local_block, 0)

    def absorb(block):
        decay = unpack_decay(block[STATE:PACK])
        cur_s[...] = decay * cur_s[...] + block[0:STATE].astype(F32)
        cur_a[...] = decay * cur_a[...]

    def row_total(mb, carry):
        cur_s[...] = jnp.zeros_like(cur_s)
        cur_a[...] = jnp.ones_like(cur_a)
        for source in range(row_len):

            @pl.when(my_x == source)
            def _():
                pre_s[mb] = cur_s[...]
                pre_a[mb] = cur_a[...]

            @pl.when(my_x != source)
            def _():
                row_arrival(source, mb).wait_recv()

            absorb(pkx[source, mb])
        tpk[mb, 0:STATE] = cur_s[...].astype(BF16)
        tpk[mb, STATE:PACK] = pack_decay(cur_a[...])
        for dest in range(1, col_len):

            @pl.when(dest > my_y)
            def _():
                col_copy(dest, mb).start()

        return carry

    lax.fori_loop(0, MB, row_total, 0)

    def finish_scan(mb, carry):
        cur_s[...] = jnp.zeros_like(cur_s)
        for source in range(col_len - 1):

            @pl.when(source < my_y)
            def _():
                col_arrival(source, mb).wait_recv()
                absorb(pky[source, mb])

        entering = (pre_a[mb] * cur_s[...] + pre_s[mb]).astype(BF16)
        from_state = jnp.dot(cs[mb], entering, preferred_element_type=F32)
        results = lo[mb] + ce[mb] * from_state
        gate = acc[mb, :, width:] * ss[mb]
        gated = results * (gate * sigmoid(gate))
        square = jnp.sum(gated * gated, axis=1, keepdims=True)
        sq[pl.ds(mb, 1), :] = jnp.broadcast_to(square, (TOK, TOK)).T[0:1]
        gb[mb] = (gated * inner_gain[...].astype(F32)).astype(BF16)
        return carry

    sq[...] = jnp.zeros_like(sq)
    lax.fori_loop(0, MB, finish_scan, 0)

    def square_copy(d):
        return remote(sq, sqr.at[me], q_s.at[d], q_r.at[me], to_mp(d))

    def square_arrival(d):
        return remote(sq, sqr.at[at_mp(d)], q_s.at[d], q_r.at[at_mp(d)], to_mp(d))

    for d in range(1, size):
        square_copy(d).start()

    out_copy.wait()
    pairs = size // 2
    my_pair = lax.div(me, 2)
    for i in range(pairs):
        pair = lax.rem(my_pair + (pairs // 2 + i), pairs)
        start = pl.multiple_of(pair * (2 * local), TOK)
        term = jnp.dot(
            gb[...].reshape(MB * TOK, width),
            wo[:, pl.ds(start, 2 * local)],
            preferred_element_type=F32,
        ).astype(BF16)
        for half in range(2):
            upd[2 * pair + half] = term[:, half * local : (half + 1) * local].reshape(
                MB, TOK, local
            )

    def scatter_copy(side, step, mb):
        if side > 0:
            bank, mine, send, recv, rel = rr, sr, rsr_s, rsr_r, far
        else:
            bank, mine, send, recv, rel = rl, sl, rsl_s, rsl_r, -near
        src = upd.at[at_mp(rel), mb] if step == 0 else mine.at[step - 1, mb]
        return remote(
            src, bank.at[step, mb], send.at[step, mb], recv.at[step, mb], to_mp(side)
        )

    def add_term(bank, step, mb, rel):
        return bank[step, mb].astype(F32) + upd[at_mp(rel), mb].astype(F32)

    for mb in range(MB):
        scatter_copy(1, 0, mb).start()
        scatter_copy(-1, 0, mb).start()
    for step in range(1, far):
        for mb in range(MB):
            scatter_copy(1, step - 1, mb).wait_recv()
            sr[step - 1, mb] = add_term(rr, step - 1, mb, far - step).astype(BF16)
            scatter_copy(1, step, mb).start()
            if step < near:
                scatter_copy(-1, step - 1, mb).wait_recv()
                sl[step - 1, mb] = add_term(rl, step - 1, mb, step - near).astype(BF16)
                scatter_copy(-1, step, mb).start()

    for d in range(1, size):
        square_arrival(d).wait_recv()
    sqr[me] = sq[...]
    squares = sqr[0]
    for j in range(1, size):
        squares = squares + sqr[j]

    for mb in range(MB):
        if near > 0:
            scatter_copy(-1, near - 1, mb).wait_recv()
        scatter_copy(1, far - 1, mb).wait_recv()
        total = add_term(rr, far - 1, mb, 0)
        if near > 0:
            total = total + rl[near - 1, mb].astype(F32)
        mean = spread(squares[mb : mb + 1]).T[:, 0:1] / (size * width)
        out[0, mb] = (xin[mb].astype(F32) + total * lax.rsqrt(mean + EPS)).astype(BF16)

        @pl.when(section == 0)
        def _():
            pass_on[mb].start()

    for mb in range(MB):

        @pl.when(section == 0)
        def _():
            pass_on[mb].wait_send()

        for step in range(far):
            gather_copy(1, step, mb).wait_send()
            scatter_copy(1, step, mb).wait_send()
        for step in range(near):
            gather_copy(-1, step, mb).wait_send()
            scatter_copy(-1, step, mb).wait_send()

        @pl.when(seq < seq_len - 1)
        def _():
            halo_copy(mb).wait_send()

        for d in range(1, row_len):
            row_copy(lax.rem(my_x + d, row_len), mb).wait_send()
        for dest in range(1, col_len):

            @pl.when(dest > my_y)
            def _():
                col_copy(dest, mb).wait_send()

    for d in range(1, size):
        square_copy(d).wait_send()

    @pl.when(seq < seq_len - 1)
    def _():
        doc_copy.wait_send()


def per_device(
    stream,
    segment_ids,
    norm_gain,
    in_weight,
    bc_weight,
    dt_weight,
    dt_bias,
    decay_rate,
    conv_inner,
    conv_state,
    skip_gain,
    inner_gain,
    out_weight,
):
    size = lax.axis_size("mp")
    seq_len = lax.axis_size("seq")
    row_len = math.isqrt(seq_len)
    col_len = seq_len // row_len
    local = stream.shape[-1]
    depth = in_weight.shape[1]
    width = in_weight.shape[-1]
    heads = width // HDIM
    states = bc_weight.shape[-1]
    far = size // 2
    near = max(size - 1 - far, 1)
    whole = pl.BlockSpec(memory_space=pltpu.VMEM)
    apart = pl.BlockSpec(memory_space=pl.ANY)
    part = (MB, TOK, local)
    dma = pltpu.SemaphoreType.DMA
    scratch = [
        pltpu.VMEM(part, BF16),
        pltpu.VMEM((far, *part), BF16),
        pltpu.VMEM((near, *part), BF16),
        pltpu.VMEM((depth, 2 * width), BF16),
        pltpu.VMEM((depth, states), BF16),
        pltpu.VMEM((depth, heads), BF16),
        pltpu.VMEM(out_weight.shape[1:], BF16),
        pltpu.VMEM((size, local), F32),
        pltpu.VMEM((MB, TOK, 2 * width), F32),
        pltpu.VMEM((MB, TOK, states), F32),
        pltpu.VMEM((MB, TOK, heads), F32),
        pltpu.VMEM((MB, TOK, 1), F32),
        pltpu.VMEM((MB, TOK, width + states), BF16),
        pltpu.VMEM((MB, LAG, width + states), BF16),
        pltpu.VMEM((MB, TOK), jnp.int32),
        pltpu.VMEM((LAG + TOK, width + states), F32),
        pltpu.VMEM((LAG + TOK, TOK), F32),
        pltpu.VMEM((MB, TOK, width), BF16),
        pltpu.VMEM((MB, TOK, STATE), BF16),
        pltpu.VMEM((MB, TOK, heads), F32),
        pltpu.VMEM((MB, TOK, TOK), F32),
        pltpu.VMEM((MB, TOK, TOK), F32),
        pltpu.VMEM((MB, TOK, width), F32),
        pltpu.VMEM((MB, TOK, width), F32),
        pltpu.VMEM((row_len, MB, PACK, width), BF16),
        pltpu.VMEM((col_len, MB, PACK, width), BF16),
        pltpu.VMEM((MB, PACK, width), BF16),
        pltpu.VMEM((STATE, width), F32),
        pltpu.VMEM((1, width), F32),
        pltpu.VMEM((MB, STATE, width), F32),
        pltpu.VMEM((MB, 1, width), F32),
        pltpu.VMEM((MB, TOK, width), BF16),
        pltpu.VMEM((8, TOK), F32),
        pltpu.VMEM((size, 8, TOK), F32),
        pltpu.VMEM((size, *part), BF16),
        pltpu.VMEM((far, *part), BF16),
        pltpu.VMEM((near, *part), BF16),
        pltpu.VMEM((far, *part), BF16),
        pltpu.VMEM((near, *part), BF16),
        dma((size, 3)),
        dma((2,)),
        dma((far, MB)),
        dma((far, MB)),
        dma((near, MB)),
        dma((near, MB)),
        dma((MB,)),
        dma((MB,)),
        dma,
        dma,
        dma((row_len, MB)),
        dma((row_len, MB)),
        dma((col_len, MB)),
        dma((col_len, MB)),
        dma((size,)),
        dma((size,)),
        dma((far, MB)),
        dma((far, MB)),
        dma((near, MB)),
        dma((near, MB)),
        dma((MB,)),
        dma((MB,)),
    ]
    return pl.pallas_call(
        functools.partial(kernel, size, row_len, seq_len),
        out_shape=jax.ShapeDtypeStruct((1, *part), BF16),
        in_specs=[
            apart,
            whole,
            whole,
            apart,
            apart,
            apart,
            whole,
            whole,
            whole,
            whole,
            whole,
            whole,
            apart,
        ],
        out_specs=whole,
        scratch_shapes=scratch,
        compiler_params=pltpu.CompilerParams(
            collective_id=0, has_side_effects=True, vmem_limit_bytes=60 << 20
        ),
        name="mixer_layers",
    )(
        stream,
        segment_ids,
        norm_gain,
        in_weight[0].reshape(depth, 2 * width),
        bc_weight[0],
        dt_weight[0],
        dt_bias,
        decay_rate,
        conv_inner,
        conv_state,
        skip_gain,
        inner_gain,
        out_weight[0],
    )


def solution(mesh):
    placed = (
        P(None, "seq", "mp"),
        P(None, "seq"),
        P("section", None),
        P("section", None, None, "mp"),
        P("section", None, None),
        P("section", None, "mp"),
        P("section", "mp"),
        P("section", "mp"),
        P("section", None, "mp"),
        P("section", None, None),
        P("section", "mp"),
        P("section", "mp"),
        P("section", "mp", None),
    )
    return jax.shard_map(
        per_device,
        mesh=mesh,
        in_specs=placed,
        out_specs=P("section", None, "seq", "mp"),
        check_vma=False,
    )
```

```python
import functools
import math

import jax
import jax.numpy as jnp
from jax import lax
from jax.experimental import pallas as pl
from jax.experimental.pallas import tpu as pltpu
from jax.sharding import PartitionSpec as P

HDIM = 64
STATE = 64
EPS = 1e-05
F32 = jnp.float32
BF16 = jnp.bfloat16
HIGH = lax.Precision.HIGHEST
TOK = 128
MB = 2
LAG = 16
PACK = STATE + 16
SUB = 2


def spread(row):
    return jnp.broadcast_to(row, (TOK, TOK))


def sigmoid(value):
    return 1.0 / (1.0 + jnp.exp(-value))


def kernel(
    size,
    row_len,
    seq_len,
    stream,
    seg,
    norm_gain,
    w_in,
    w_bc,
    w_dt,
    dt_bias,
    decay_rate,
    conv_inner,
    conv_state,
    skip_gain,
    inner_gain,
    w_out,
    out,
    xin,
    gr,
    gl,
    wraw,
    wi,
    wb,
    wd,
    wo,
    wot,
    gains,
    acc,
    accs,
    accd,
    ss,
    rows_scale,
    cols_scale,
    jn,
    halo,
    prev,
    pad,
    dpad,
    us,
    cs,
    cums,
    flats,
    inter,
    lo,
    ce,
    pkx,
    pky,
    tpk,
    cur_s,
    cur_a,
    pre_s,
    pre_a,
    gb,
    sq,
    sqr,
    upd,
    rr,
    rl,
    sr,
    sl,
    w_sem,
    x_sem,
    agr_s,
    agr_r,
    agl_s,
    agl_r,
    h_s,
    h_r,
    d_s,
    d_r,
    px_s,
    px_r,
    py_s,
    py_r,
    q_s,
    q_r,
    rsr_s,
    rsr_r,
    rsl_s,
    rsl_r,
    sx_s,
    sx_r,
):
    local = stream.shape[1]
    piece = local // SUB
    width = wo.shape[0]
    heads = width // HDIM
    state_at = width
    col_len = seq_len // row_len
    far = size // 2
    near = size - 1 - far
    section = lax.axis_index("section")
    seq = lax.axis_index("seq")
    me = lax.axis_index("mp")
    my_x = lax.rem(seq, row_len)
    my_y = lax.div(seq, row_len)

    def at_mp(index):
        return lax.rem(me + index + 2 * size, size)

    def to_mp(index):
        return {"mp": at_mp(index)}

    def remote(src, dst, send, recv, where):
        return pltpu.make_async_remote_copy(
            src_ref=src,
            dst_ref=dst,
            send_sem=send,
            recv_sem=recv,
            device_id=where,
            device_id_type=pl.DeviceIdType.MESH,
        )

    order = [0]
    for step in range(1, far + 1):
        order.append(-step)
        if step <= near:
            order.append(step)
    slot_of = {rel: index for index, rel in enumerate(order)}

    def rows_of(rel):
        return pl.ds(pl.multiple_of(at_mp(rel) * local, 64), local)

    def weight_copies(rel):
        rows = rows_of(rel)
        k = slot_of[rel]
        return [
            pltpu.make_async_copy(w_in.at[rows], wraw.at[rows], w_sem.at[k, 0]),
            pltpu.make_async_copy(w_bc.at[rows], wb.at[rows], w_sem.at[k, 1]),
        ]

    out_copy = pltpu.make_async_copy(w_out, wo, x_sem.at[1])
    for rel in order:
        for copy in weight_copies(rel):
            copy.start()
    out_copy.start()
    first_copy = pltpu.make_async_copy(stream, xin, x_sem.at[0])

    @pl.when(section == 0)
    def _():
        first_copy.start()

    barrier = pltpu.get_barrier_semaphore()
    partners = [to_mp(d) for d in range(1, size)]
    partners += [
        {"seq": my_y * row_len + lax.rem(my_x + d, row_len)} for d in range(1, row_len)
    ]
    partners += [
        {"seq": lax.rem(my_y + d, col_len) * row_len + my_x} for d in range(1, col_len)
    ]
    partners += [{"seq": lax.rem(seq + d, seq_len)} for d in (1, seq_len - 1)]
    partners += [{"section": 1 - section}]
    for where in partners:
        pl.semaphore_signal(
            barrier, inc=1, device_id=where, device_id_type=pl.DeviceIdType.MESH
        )
    pl.semaphore_wait(barrier, len(partners))

    doc_copy = remote(seg, prev, d_s, d_r, {"seq": lax.rem(seq + 1, seq_len)})

    @pl.when(seq < seq_len - 1)
    def _():
        doc_copy.start()

    @pl.when(seq == 0)
    def _():
        prev[...] = jnp.zeros_like(prev)
        halo[...] = jnp.zeros_like(halo)

    for j in range(size):
        lanes = slice(j * local, (j + 1) * local)
        gain = norm_gain[0:1, lanes].astype(F32)
        gains[j : j + 1, :] = gain
        wd[j] = (w_dt[:, lanes].astype(F32) * gain).astype(BF16)

    pass_on = [
        remote(out.at[0, mb], xin.at[mb], sx_s.at[mb], sx_r.at[mb], {"section": 1 - section})
        for mb in range(MB)
    ]

    @pl.when(section == 0)
    def _():
        first_copy.wait()

    def hops(side, mb):
        return far if (side > 0) == (mb == 0) else near

    def cut(part):
        return pl.ds(part * piece, piece)

    def gather_copy(side, step, mb, part):
        bank, send, recv = (gr, agr_s, agr_r) if side > 0 else (gl, agl_s, agl_r)
        src = xin.at[mb, cut(part)] if step == 0 else bank.at[step - 1, mb, cut(part)]
        return remote(
            src,
            bank.at[step, mb, cut(part)],
            send.at[step, mb, part],
            recv.at[step, mb, part],
            to_mp(side),
        )

    def project(blocks, rel, first):
        for copy in weight_copies(rel):
            copy.wait()
        owner = at_mp(rel)
        rows = rows_of(rel)
        halves = pltpu.einshape("ksl->skl", wraw[rows])
        wi[:, :width] = halves[0]
        wi[:, width:] = halves[1]
        gain = gains[pl.ds(owner, 1), :]
        lhs = []
        for mb, block in enumerate(blocks):
            wide = block.astype(F32)
            square = jnp.sum(wide * wide, axis=0, keepdims=True)
            step_raw = jnp.dot(wd[owner], block, preferred_element_type=F32)
            if first:
                ss[mb : mb + 1] = square
                accd[mb] = step_raw
            else:
                ss[mb : mb + 1] += square
                accd[mb] += step_raw
            lhs.append((block.T.astype(F32) * gain).astype(BF16))
        scaled = jnp.concatenate(lhs, axis=0)
        block = 256
        pieces = [
            (acc, n * block, wi[:, n * block : (n + 1) * block])
            for n in range(2 * width // block)
        ]
        pieces += [(accs, 0, wb[rows, :])]
        for total, start, weight in pieces:
            count = weight.shape[1]
            term = jnp.dot(scaled, weight, preferred_element_type=F32).reshape(MB, TOK, count)
            if first:
                total[:, :, start : start + count] = term
            else:
                total[:, :, start : start + count] += term

    def turn(first, count):
        for c in range(first, first + count):
            wot[c * TOK : (c + 1) * TOK, :] = wo[:, c * TOK : (c + 1) * TOK].T

    for mb in range(MB):

        @pl.when(section == 1)
        def _():
            pass_on[mb].wait_recv()

        for part in range(SUB):
            for side in (1, -1):
                if hops(side, mb) > 0:
                    gather_copy(side, 0, mb, part).start()
    project([xin[mb] for mb in range(MB)], 0, True)
    out_copy.wait()
    turns = size * local // TOK // far
    for step in range(far):
        for part in range(SUB):
            for mb in range(MB):
                for side in (1, -1):
                    if step < hops(side, mb):
                        gather_copy(side, step, mb, part).wait_recv()
                    if step + 1 < hops(side, mb):
                        gather_copy(side, step + 1, mb, part).start()
        if step < near:
            project([gr[step, mb] for mb in range(MB)], -1 - step, False)
            project([gl[step, mb] for mb in range(MB)], 1 + step, False)
        else:
            project([gr[step, 0], gl[step, 1]], -1 - step, False)
        turn(step * turns, turns)

    def halo_copy(mb):
        return remote(
            jn.at[mb, TOK - LAG : TOK],
            halo.at[mb],
            h_s.at[mb],
            h_r.at[mb],
            {"seq": lax.rem(seq + 1, seq_len)},
        )

    def join(mb, carry):
        row = lax.rsqrt(ss[pl.ds(mb, 1), :] / (size * local) + EPS)
        scale = spread(row).T[:, 0:1]
        rows_scale[pl.ds(mb, 1), :] = row
        cols_scale[mb] = scale
        jn[mb, :, :width] = (acc[mb, :, :width] * scale).astype(BF16)
        jn[mb, :, width:] = (accs[mb] * scale).astype(BF16)

        @pl.when(seq < seq_len - 1)
        def _():
            halo_copy(mb).start()

        return carry

    lax.fori_loop(0, MB, join, 0)

    spread_heads = (
        lax.broadcasted_iota(jnp.int32, (heads, width), 1) // HDIM
        == lax.broadcasted_iota(jnp.int32, (heads, width), 0)
    ).astype(F32)

    def expand(value):
        return jnp.dot(value, spread_heads, precision=HIGH, preferred_element_type=F32)

    def pack_decay(decay):
        high = decay.astype(BF16).astype(F32)
        low = decay - high
        index = lax.broadcasted_iota(jnp.int32, (LAG, width), 0)
        return jnp.where(index == 0, high, jnp.where(index == 1, low, 0.0)).astype(BF16)

    def unpack_decay(block):
        both = block.astype(F32)
        return both[0:1] + both[1:2]

    def row_copy(dest, mb):
        return remote(
            pkx.at[my_x, mb],
            pkx.at[my_x, mb],
            px_s.at[dest, mb],
            px_r.at[my_x, mb],
            {"seq": my_y * row_len + dest},
        )

    def row_arrival(source, mb):
        return remote(
            pkx.at[source, mb],
            pkx.at[source, mb],
            px_s.at[source, mb],
            px_r.at[source, mb],
            {"seq": my_y * row_len + source},
        )

    def col_copy(dest, mb):
        return remote(
            tpk.at[mb],
            pky.at[my_y, mb],
            py_s.at[dest, mb],
            py_r.at[my_y, mb],
            {"seq": dest * row_len + my_x},
        )

    def col_arrival(source, mb):
        return remote(
            tpk.at[mb],
            pky.at[source, mb],
            py_s.at[source, mb],
            py_r.at[source, mb],
            {"seq": source * row_len + my_x},
        )

    same = lax.broadcasted_iota(jnp.int32, (heads, heads), 0) == lax.broadcasted_iota(
        jnp.int32, (heads, heads), 1
    )

    def stand(row):
        return jnp.sum(jnp.where(same, row, 0.0), axis=1, keepdims=True)

    bias = stand(dt_bias[...])
    rate = stand(decay_rate[...])

    @pl.when(seq > 0)
    def _():
        doc_copy.wait_recv()

    def scan_block(mb, carry):
        own_row = spread(seg[pl.ds(mb, 1), :].astype(F32))
        own_col = own_row.T
        old_col = spread(prev[pl.ds(mb, 1), :].astype(F32)).T
        dpad[0:LAG] = old_col[TOK - LAG : TOK]
        dpad[LAG : LAG + TOK] = own_col
        doc = own_col[:, 0:1]
        prior = old_col[TOK - 1 : TOK, 0:1]
        last = own_col[TOK - 1 : TOK, 0:1]

        raw = accd[mb] * rows_scale[pl.ds(mb, 1), :] + bias
        steps_flat = jnp.maximum(raw, 0.0) + jnp.log1p(jnp.exp(-jnp.abs(raw)))
        places_t = lax.broadcasted_iota(jnp.int32, (TOK, TOK), 0)
        places_s = lax.broadcasted_iota(jnp.int32, (TOK, TOK), 1)
        lower = places_t >= places_s
        cum_flat = jnp.dot(
            -steps_flat * rate,
            (places_t <= places_s).astype(F32),
            precision=HIGH,
            preferred_element_type=F32,
        )
        flat = jnp.concatenate(
            [cum_flat, steps_flat, jnp.zeros((TOK - 2 * heads, TOK), F32)], axis=0
        )
        flats[mb] = flat
        stood = flat.T
        cumlog = stood[:, 0:heads]
        steps_dt = stood[:, heads : 2 * heads]
        cums[mb] = cumlog
        tail = jnp.where(doc == last, jnp.exp(cumlog[TOK - 1 : TOK] - cumlog), 0.0) * steps_dt
        carry_in = jnp.where(doc == prior, jnp.exp(cumlog), 0.0)
        tail_wide = expand(tail)
        carry_wide = expand(carry_in)
        ce[mb] = carry_wide

        @pl.when(seq > 0)
        def _():
            halo_copy(mb).wait_recv()

        pad[0:LAG] = halo[mb].astype(F32)
        pad[LAG : LAG + TOK] = jn[mb].astype(F32)
        taps = conv_inner.shape[1]
        matches = [
            dpad[LAG - taps + 1 + k : LAG - taps + 1 + k + TOK] == own_col for k in range(taps)
        ]
        mixed = []
        for j in range(pad.shape[1] // TOK):
            lanes = slice(j * TOK, (j + 1) * TOK)
            if j * TOK < state_at:
                tap = conv_inner[0, :, lanes]
            else:
                tap = conv_state[0, :, j * TOK - state_at : (j + 1) * TOK - state_at]
            total = jnp.zeros((TOK, TOK), F32)
            for k in range(taps):
                start = LAG - taps + 1 + k
                term = pad[start : start + TOK, lanes] * tap[k : k + 1]
                total = total + jnp.where(matches[k], term, 0.0)
            mixed.append(total * sigmoid(total))
        inputs = [part.astype(BF16) for part in mixed[:-1]]
        both = mixed[-1].astype(BF16).astype(F32)
        b_cols = both.T[0:STATE].astype(BF16)
        c_rows = pltpu.roll(both, STATE, axis=1)[:, 0:STATE].astype(BF16)
        cs[mb] = c_rows
        for j, part in enumerate(inputs):
            lanes = slice(j * TOK, (j + 1) * TOK)
            us[mb, :, lanes] = part
            weighted = (part.astype(F32) * tail_wide[:, lanes]).astype(BF16)
            pkx[my_x, mb, 0:STATE, lanes] = jnp.dot(
                b_cols, weighted, preferred_element_type=F32
            ).astype(BF16)
        pkx[my_x, mb, STATE:PACK, :] = pack_decay(carry_wide[TOK - 1 : TOK])
        for d in range(1, row_len):
            row_copy(lax.rem(my_x + d, row_len), mb).start()
        inter[mb] = jnp.where(
            lower & (own_col == own_row),
            jnp.dot(c_rows, b_cols, preferred_element_type=F32),
            0.0,
        )
        return carry

    lax.fori_loop(0, MB, scan_block, 0)
    skip_wide = expand(skip_gain[...])

    def local_block(mb, carry):
        own_row = spread(seg[pl.ds(mb, 1), :].astype(F32))
        lower = lax.broadcasted_iota(jnp.int32, (TOK, TOK), 0) >= lax.broadcasted_iota(
            jnp.int32, (TOK, TOK), 1
        )
        keep = lower & (own_row.T == own_row)
        left = lax.broadcasted_iota(jnp.int32, (TOK, TOK), 1) < HDIM
        cross = inter[mb]
        for j in range(width // TOK):
            lanes = slice(j * TOK, (j + 1) * TOK)
            mixing = []
            for h in (2 * j, 2 * j + 1):
                gap = cums[mb, :, h : h + 1] - flats[mb, h : h + 1, :]
                decays = jnp.exp(jnp.where(keep, gap, -1e30))
                mixing.append(
                    (decays * cross * flats[mb, heads + h : heads + h + 1, :]).astype(BF16)
                )
            part = us[mb, :, lanes]
            zero = jnp.zeros_like(part)
            stacked = jnp.concatenate(
                [jnp.where(left, part, zero), jnp.where(left, zero, part)], axis=0
            )
            lo[mb, :, lanes] = (
                jnp.dot(
                    jnp.concatenate(mixing, axis=1), stacked, preferred_element_type=F32
                )
                + skip_wide[:, lanes] * part.astype(F32)
            )
        return carry

    lax.fori_loop(0, MB, local_block, 0)

    def absorb(block):
        decay = unpack_decay(block[STATE:PACK])
        cur_s[...] = decay * cur_s[...] + block[0:STATE].astype(F32)
        cur_a[...] = decay * cur_a[...]

    def row_total(mb, carry):
        cur_s[...] = jnp.zeros_like(cur_s)
        cur_a[...] = jnp.ones_like(cur_a)
        for source in range(row_len):

            @pl.when(my_x == source)
            def _():
                pre_s[mb] = cur_s[...]
                pre_a[mb] = cur_a[...]

            @pl.when(my_x != source)
            def _():
                row_arrival(source, mb).wait_recv()

            absorb(pkx[source, mb])
        tpk[mb, 0:STATE] = cur_s[...].astype(BF16)
        tpk[mb, STATE:PACK] = pack_decay(cur_a[...])
        for dest in range(1, col_len):

            @pl.when(dest > my_y)
            def _():
                col_copy(dest, mb).start()

        return carry

    lax.fori_loop(0, MB, row_total, 0)

    def finish_scan(mb, carry):
        cur_s[...] = jnp.zeros_like(cur_s)
        for source in range(col_len - 1):

            @pl.when(source < my_y)
            def _():
                col_arrival(source, mb).wait_recv()
                absorb(pky[source, mb])

        entering = (pre_a[mb] * cur_s[...] + pre_s[mb]).astype(BF16)
        from_state = jnp.dot(cs[mb], entering, preferred_element_type=F32)
        results = lo[mb] + ce[mb] * from_state
        gate = acc[mb, :, width:] * cols_scale[mb]
        gated = results * (gate * sigmoid(gate))
        square = jnp.sum(gated * gated, axis=1, keepdims=True)
        sq[pl.ds(mb, 1), :] = jnp.broadcast_to(square, (TOK, TOK)).T[0:1]
        gb[mb] = (gated * inner_gain[...].astype(F32)).astype(BF16)
        return carry

    sq[...] = jnp.zeros_like(sq)
    lax.fori_loop(0, MB, finish_scan, 0)

    def square_copy(d):
        return remote(sq, sqr.at[me], q_s.at[d], q_r.at[me], to_mp(d))

    def square_arrival(d):
        return remote(sq, sqr.at[at_mp(d)], q_s.at[d], q_r.at[at_mp(d)], to_mp(d))

    for d in range(1, size):
        square_copy(d).start()

    gated_all = gb[...].reshape(MB * TOK, width)

    def produce(rel):
        term = lax.dot_general(
            wot[rows_of(rel), :],
            gated_all,
            (((1,), (1,)), ((), ())),
            preferred_element_type=F32,
        ).astype(BF16)
        for mb in range(MB):
            upd[at_mp(rel), mb] = term[:, mb * TOK : (mb + 1) * TOK]

    def scatter_copy(side, step, mb, part):
        if side > 0:
            bank, mine, send, recv = rr, sr, rsr_s, rsr_r
        else:
            bank, mine, send, recv = rl, sl, rsl_s, rsl_r
        rel = side * (hops(side, mb) - step)
        src = upd.at[at_mp(rel), mb] if step == 0 else mine.at[step - 1, mb]
        return remote(
            src.at[cut(part)],
            bank.at[step, mb, cut(part)],
            send.at[step, mb, part],
            recv.at[step, mb, part],
            to_mp(side),
        )

    def add_term(bank, step, mb, part, rel):
        rows = cut(part)
        return bank[step, mb, rows].astype(F32) + upd[at_mp(rel), mb, rows].astype(F32)

    produce(far)
    for part in range(SUB):
        for mb in range(MB):
            scatter_copy(1 if mb == 0 else -1, 0, mb, part).start()
    for rel in (near, -near) if near > 0 else ():
        produce(rel)
        for part in range(SUB):
            scatter_copy(1 if rel > 0 else -1, 0, 1 if rel > 0 else 0, part).start()
    for rel in range(near - 1, 0, -1):
        produce(rel)
        produce(-rel)
    produce(0)
    for step in range(1, far):
        for part in range(SUB):
            for mb in range(MB):
                for side, bank, mine in ((1, rr, sr), (-1, rl, sl)):
                    if step < hops(side, mb):
                        scatter_copy(side, step - 1, mb, part).wait_recv()
                        rel = side * (hops(side, mb) - step)
                        mine[step - 1, mb, cut(part)] = add_term(
                            bank, step - 1, mb, part, rel
                        ).astype(BF16)
                        scatter_copy(side, step, mb, part).start()

    for d in range(1, size):
        square_arrival(d).wait_recv()
    sqr[me] = sq[...]
    squares = sqr[0]
    for j in range(1, size):
        squares = squares + sqr[j]

    for mb in range(MB):
        factor = lax.rsqrt(squares[mb : mb + 1] / (size * width) + EPS)
        main, other = (1, -1) if mb == 0 else (-1, 1)
        first_bank, last_bank = (rl, rr) if mb == 0 else (rr, rl)
        for part in range(SUB):
            if near > 0:
                scatter_copy(other, near - 1, mb, part).wait_recv()
            scatter_copy(main, far - 1, mb, part).wait_recv()
            total = add_term(last_bank, far - 1, mb, part, 0)
            if near > 0:
                total = total + first_bank[near - 1, mb, cut(part)].astype(F32)
            out[0, mb, cut(part)] = (
                xin[mb, cut(part)].astype(F32) + total * factor
            ).astype(BF16)

        @pl.when(section == 0)
        def _():
            pass_on[mb].start()

    for mb in range(MB):

        @pl.when(section == 0)
        def _():
            pass_on[mb].wait_send()

        for part in range(SUB):
            for side in (1, -1):
                for step in range(hops(side, mb)):
                    gather_copy(side, step, mb, part).wait_send()
                    scatter_copy(side, step, mb, part).wait_send()

        @pl.when(seq < seq_len - 1)
        def _():
            halo_copy(mb).wait_send()

        for d in range(1, row_len):
            row_copy(lax.rem(my_x + d, row_len), mb).wait_send()
        for dest in range(1, col_len):

            @pl.when(dest > my_y)
            def _():
                col_copy(dest, mb).wait_send()

    for d in range(1, size):
        square_copy(d).wait_send()

    @pl.when(seq < seq_len - 1)
    def _():
        doc_copy.wait_send()


def per_device(
    stream,
    segment_ids,
    norm_gain,
    in_weight,
    bc_weight,
    dt_weight,
    dt_bias,
    decay_rate,
    conv_inner,
    conv_state,
    skip_gain,
    inner_gain,
    out_weight,
):
    size = lax.axis_size("mp")
    seq_len = lax.axis_size("seq")
    row_len = math.isqrt(seq_len)
    col_len = seq_len // row_len
    local = stream.shape[-1]
    depth = in_weight.shape[1]
    width = in_weight.shape[-1]
    heads = width // HDIM
    states = bc_weight.shape[-1]
    far = size // 2
    whole = pl.BlockSpec(memory_space=pltpu.VMEM)
    apart = pl.BlockSpec(memory_space=pl.ANY)
    part = (MB, local, TOK)
    dma = pltpu.SemaphoreType.DMA
    scratch = [
        pltpu.VMEM(part, BF16),
        pltpu.VMEM((far, *part), BF16),
        pltpu.VMEM((far, *part), BF16),
        pltpu.VMEM((depth, 2, width), BF16),
        pltpu.VMEM((local, 2 * width), BF16),
        pltpu.VMEM((depth, states), BF16),
        pltpu.VMEM((size, heads, local), BF16),
        pltpu.VMEM(out_weight.shape[1:], BF16),
        pltpu.VMEM((depth, width), BF16),
        pltpu.VMEM((size, local), F32),
        pltpu.VMEM((MB, TOK, 2 * width), F32),
        pltpu.VMEM((MB, TOK, states), F32),
        pltpu.VMEM((MB, heads, TOK), F32),
        pltpu.VMEM((MB, TOK), F32),
        pltpu.VMEM((MB, TOK), F32),
        pltpu.VMEM((MB, TOK, 1), F32),
        pltpu.VMEM((MB, TOK, width + states), BF16),
        pltpu.VMEM((MB, LAG, width + states), BF16),
        pltpu.VMEM((MB, TOK), jnp.int32),
        pltpu.VMEM((LAG + TOK, width + states), F32),
        pltpu.VMEM((LAG + TOK, TOK), F32),
        pltpu.VMEM((MB, TOK, width), BF16),
        pltpu.VMEM((MB, TOK, STATE), BF16),
        pltpu.VMEM((MB, TOK, heads), F32),
        pltpu.VMEM((MB, TOK, TOK), F32),
        pltpu.VMEM((MB, TOK, TOK), F32),
        pltpu.VMEM((MB, TOK, width), F32),
        pltpu.VMEM((MB, TOK, width), F32),
        pltpu.VMEM((row_len, MB, PACK, width), BF16),
        pltpu.VMEM((col_len, MB, PACK, width), BF16),
        pltpu.VMEM((MB, PACK, width), BF16),
        pltpu.VMEM((STATE, width), F32),
        pltpu.VMEM((1, width), F32),
        pltpu.VMEM((MB, STATE, width), F32),
        pltpu.VMEM((MB, 1, width), F32),
        pltpu.VMEM((MB, TOK, width), BF16),
        pltpu.VMEM((8, TOK), F32),
        pltpu.VMEM((size, 8, TOK), F32),
        pltpu.VMEM((size, *part), BF16),
        pltpu.VMEM((far, *part), BF16),
        pltpu.VMEM((far, *part), BF16),
        pltpu.VMEM((far, *part), BF16),
        pltpu.VMEM((far, *part), BF16),
        dma((size, 2)),
        dma((2,)),
        dma((far, MB, SUB)),
        dma((far, MB, SUB)),
        dma((far, MB, SUB)),
        dma((far, MB, SUB)),
        dma((MB,)),
        dma((MB,)),
        dma,
        dma,
        dma((row_len, MB)),
        dma((row_len, MB)),
        dma((col_len, MB)),
        dma((col_len, MB)),
        dma((size,)),
        dma((size,)),
        dma((far, MB, SUB)),
        dma((far, MB, SUB)),
        dma((far, MB, SUB)),
        dma((far, MB, SUB)),
        dma((MB,)),
        dma((MB,)),
    ]
    result = pl.pallas_call(
        functools.partial(kernel, size, row_len, seq_len),
        out_shape=jax.ShapeDtypeStruct((1, *part), BF16),
        in_specs=[
            apart,
            whole,
            whole,
            apart,
            apart,
            whole,
            whole,
            whole,
            whole,
            whole,
            whole,
            whole,
            apart,
        ],
        out_specs=whole,
        scratch_shapes=scratch,
        compiler_params=pltpu.CompilerParams(
            collective_id=0, has_side_effects=True, vmem_limit_bytes=60 << 20
        ),
        name="mixer_layers",
    )(
        stream.transpose(0, 2, 1),
        segment_ids,
        norm_gain,
        in_weight[0],
        bc_weight[0],
        dt_weight[0].T,
        dt_bias,
        decay_rate,
        conv_inner,
        conv_state,
        skip_gain,
        inner_gain,
        out_weight[0],
    )
    return result.transpose(0, 1, 3, 2)


def solution(mesh):
    placed = (
        P(None, "seq", "mp"),
        P(None, "seq"),
        P("section", None),
        P("section", None, None, "mp"),
        P("section", None, None),
        P("section", None, "mp"),
        P("section", "mp"),
        P("section", "mp"),
        P("section", None, "mp"),
        P("section", None, None),
        P("section", "mp"),
        P("section", "mp"),
        P("section", "mp", None),
    )
    return jax.shard_map(
        per_device,
        mesh=mesh,
        in_specs=placed,
        out_specs=P("section", None, "seq", "mp"),
        check_vma=False,
    )
```
